32 devices in a mesh: inner: 4 (over x, core), outer: 8 (over z, y).
Axes of the slice: x: 2, y: 2, z: 4, core: 2. Of those that a mesh axis runs over, the one named last changes fastest.
Arguments:
- queries: bfloat16 [4096, 1024], P(('inner', 'outer')), may hold values from -6 to 6
- keys: bfloat16 [4096, 128], P(('inner', 'outer')), may hold values from -6 to 6
- values: bfloat16 [4096, 128], P(('inner', 'outer')), may hold values from -6 to 6
- out_grad: bfloat16 [4096, 1024], P(('inner', 'outer')), may hold values from -6 to 6
- forward_out: bfloat16 [4096, 1024], P(('inner', 'outer')), may hold values from -0.796875 to 0.796875
- log_sum_exp: float32 [8, 4096], P(None, ('inner', 'outer')), may hold values from 3 to 5
- span_table: int32 [64], replicated, may hold values from 0 to 63, each once
- mask_codes: int32 [32, 6], P(('inner', 'outer')), may hold values from 0 to 2
Outputs:
- query_grad: bfloat16 [4096, 1024], P(('inner', 'outer'))
- key_grad: bfloat16 [4096, 128], P(('inner', 'outer'))
- value_grad: bfloat16 [4096, 128], P(('inner', 'outer'))
The draws below stay inside these ranges and needn't reach their ends.
Inputs may be any that keep to these rules, and one draw needn't show every extreme that they name: `span_table`: each span number appears exactly once.
All inputs are finite; a program needn't handle non-finite values.
Results may differ from the reference program's by a relative error of at most 0.0057.
Values may be sent and summed in bfloat16 or wider, within the bound.
A program may use at most 64 MiB of HBM per device.

```python
import jax
import jax.numpy as jnp
from jax import lax

H = 8
DH = 128
ROWS = 128
REMOTE = 6
BLOCKS = 32
TOKENS = 4096
SPANS = 64
N_INNER = 4
N_OUTER = 8


def place_ends(result, rng, smallest, largest):
    spot = [jax.random.randint(jax.random.fold_in(rng, axis), (), 0, length) for axis, length in enumerate(result.shape)]
    widest = result.shape.index(max(result.shape))
    beside = spot[:widest] + [(spot[widest] + 1) % result.shape[widest]] + spot[widest + 1:]
    return result.at[tuple(spot)].set(smallest).at[tuple(beside)].set(largest)


def level_of(rng, extent, split, low, largest):
    factor_of, own = 1.0, jax.random.fold_in(rng, 6)
    for position, blocks in split:
        heights = jnp.exp(jax.random.uniform(jax.random.fold_in(own, position), (blocks,), jnp.float32, low / len(split), largest / len(split)))
        factor_of = factor_of * jnp.repeat(heights, extent[position] // blocks).reshape([-1 if axis == position else 1 for axis in range(len(extent))])
    return factor_of


def gaussian(stream_key, dims, deviation, reach, split=(), kind=jnp.bfloat16):
    values = deviation * jax.random.normal(stream_key, dims, jnp.float32)
    if split:
        values = values * level_of(stream_key, dims, split, -0.22, 0.18)
    return jnp.clip(values, -reach, reach).astype(kind)


def setup_inputs(seed: int = 0) -> dict:
    arg_keys = jax.random.split(jax.random.key(seed), 9)
    queries = gaussian(arg_keys[0], (TOKENS, H * DH), 1.0, 6.0, ((0, 32),))
    keys = gaussian(arg_keys[1], (TOKENS, DH), 1.0, 6.0, ((0, 32),))
    values = gaussian(arg_keys[2], (TOKENS, DH), 1.0, 6.0, ((0, 32),))
    out_grad = gaussian(arg_keys[3], (TOKENS, H * DH), 1.0, 6.0, ((0, 32),))
    forward_out = gaussian(arg_keys[4], (TOKENS, H * DH), 0.1, 0.796875, ((0, 32),))
    log_sum_exp = jnp.clip(3.0 + 2.0 * jax.random.uniform(arg_keys[5], (H, TOKENS), jnp.float32) ** level_of(arg_keys[5], (H, TOKENS), ((1, 32),), -0.2, 0.2), 3.0, 5.0)
    span_table = jax.random.permutation(arg_keys[6], SPANS).astype(jnp.int32)
    mask_codes = place_ends(jax.random.randint(arg_keys[7], (BLOCKS, REMOTE), 0, 3), jax.random.fold_in(arg_keys[7], 1), 0, 2).astype(jnp.int32)
    return dict(queries=queries, keys=keys, values=values, out_grad=out_grad, forward_out=forward_out, log_sum_exp=log_sum_exp, span_table=span_table, mask_codes=mask_codes)


WINDOW_PATH = ((0, 0), (1, 0), (2, 0), (2, 1), (3, 1), (4, 1), (4, 2))


def block_terms(queries, grads_out, log_sum_exp, delta, query_pos, key_block, value_block, key_pos, mask_code):
    head_width = key_block.shape[-1]
    score_scale = head_width ** -0.5
    row_count = queries.shape[0]
    head_count = log_sum_exp.shape[0]
    query_heads = queries.astype(jnp.float32).reshape(row_count, head_count, head_width)
    gradient_heads = grads_out.astype(jnp.float32).reshape(row_count, head_count, head_width)
    key_float = key_block.astype(jnp.float32)
    value_float = value_block.astype(jnp.float32)
    scores = jnp.einsum("qhd,kd->hqk", query_heads, key_float) * score_scale
    allowed = (mask_code == 2) | ((mask_code == 1) & (key_pos[None, :] <= query_pos[:, None]))
    probs = jnp.where(allowed[None], jnp.exp(scores - log_sum_exp[:, :, None]), 0.0)
    probs_low = lax.optimization_barrier(probs.astype(jnp.bfloat16)).astype(jnp.float32)
    value_part = jnp.einsum("hqk,qhd->kd", probs_low, gradient_heads)
    dprob = jnp.einsum("qhd,kd->hqk", gradient_heads, value_float)
    dscore = (probs * (dprob - delta[:, :, None])) * score_scale
    dscore_low = lax.optimization_barrier(dscore.astype(jnp.bfloat16)).astype(jnp.float32)
    query_part = jnp.einsum("hqk,kd->qhd", dscore_low, key_float).reshape(row_count, head_count * head_width)
    key_part = jnp.einsum("hqk,qhd->kd", dscore_low, query_heads)
    return query_part, key_part, value_part


def reference(queries, keys, values, out_grad, forward_out, log_sum_exp, span_table, mask_codes):
    inner_count = N_INNER
    outer_count = N_OUTER
    half_rows = ROWS // 2

    def by_device(array):
        return array.reshape((inner_count, outer_count, ROWS) + array.shape[1:])

    query_dev = by_device(queries)
    key_dev = by_device(keys)
    value_dev = by_device(values)
    grad_dev = by_device(out_grad)
    delta_rows = jnp.sum((out_grad.astype(jnp.float32) * forward_out.astype(jnp.float32)).reshape(TOKENS, H, DH), axis=2)
    delta_dev = by_device(delta_rows).transpose(0, 1, 3, 2)
    lse_dev = log_sum_exp.reshape(H, inner_count, outer_count, ROWS).transpose(1, 2, 0, 3)
    span_pairs = span_table.reshape(inner_count, outer_count, 2)
    offsets = jnp.arange(half_rows, dtype=jnp.int32)
    positions = (span_pairs[:, :, :, None] * half_rows + offsets).reshape(inner_count, outer_count, ROWS).astype(jnp.int32)
    codes_dev = mask_codes.reshape(inner_count, outer_count, REMOTE)

    def one_slice(inner_at):
        query_here = query_dev[inner_at]
        grad_here = grad_dev[inner_at]
        lse_here = lse_dev[inner_at]
        delta_here = delta_dev[inner_at]
        pos_here = positions[inner_at]
        query_sum = jnp.zeros((outer_count, ROWS, H * DH), jnp.float32)
        key_parts = []
        value_parts = []
        for window_step, (inner_back, outer_back) in enumerate(WINDOW_PATH):
            source = (inner_at - inner_back) % inner_count
            key_seen = jnp.roll(key_dev[source], outer_back, axis=0)
            value_seen = jnp.roll(value_dev[source], outer_back, axis=0)
            pos_seen = jnp.roll(positions[source], outer_back, axis=0)
            if window_step == 0:
                code_seen = jnp.ones((outer_count,), jnp.int32)
            else:
                code_seen = codes_dev[inner_at, :, window_step - 1]
            query_part, key_part, value_part = jax.vmap(block_terms)(
                query_here, grad_here, lse_here, delta_here, pos_here, key_seen, value_seen, pos_seen, code_seen)
            query_sum = query_sum + query_part
            key_parts.append(key_part)
            value_parts.append(value_part)
        return query_sum.astype(jnp.bfloat16), jnp.stack(key_parts), jnp.stack(value_parts)

    query_total, key_parts, value_parts = lax.map(one_slice, jnp.arange(inner_count, dtype=jnp.int32))
    key_total = jnp.zeros((inner_count, outer_count, ROWS, DH), jnp.float32)
    value_total = jnp.zeros((inner_count, outer_count, ROWS, DH), jnp.float32)
    for window_step, (inner_back, outer_back) in enumerate(WINDOW_PATH):
        key_total = key_total + jnp.roll(key_parts[:, window_step], (-inner_back, -outer_back), axis=(0, 1))
        value_total = value_total + jnp.roll(value_parts[:, window_step], (-inner_back, -outer_back), axis=(0, 1))
    return (query_total.reshape(TOKENS, H * DH),
            key_total.reshape(TOKENS, DH).astype(jnp.bfloat16),
            value_total.reshape(TOKENS, DH).astype(jnp.bfloat16))
```

```python
import functools

import jax
import jax.numpy as jnp
from jax import lax
from jax.experimental import pallas as pl
from jax.experimental.pallas import tpu as pltpu
from jax.sharding import PartitionSpec as P

WINDOW_PATH = ((0, 0), (1, 0), (2, 0), (2, 1), (3, 1), (4, 1), (4, 2))
STEP_ORDER = (1, 2, 5, 4, 3, 6)
MESH = pl.DeviceIdType.MESH


def kernel(inner_count, outer_count, q_hbm, k_hbm, v_hbm, do_hbm, o_hbm, lse_ref, span_ref, code_ref,
           dq_ref, dk_ref, dv_ref,
           q_vm, do_vm, o_vm, kv_own, kv_in, g_out, g_in, dq_acc, own_acc,
           load_sem, kv_send, kv_recv, g_send, g_recv):
    inner_at = lax.axis_index("inner")
    outer_at = lax.axis_index("outer")
    head_count, rows, width = q_vm.shape
    half = rows // 2
    scale = width ** (-0.5)
    steps = range(1, len(WINDOW_PATH))

    def device(step, sign):
        a, c = WINDOW_PATH[step]
        u = lax.rem(inner_at + (sign * a) % inner_count, inner_count)
        w = lax.rem(outer_at + (sign * c) % outer_count, outer_count)
        return u, w

    barrier = pltpu.get_barrier_semaphore()
    for step in steps:
        for sign in (1, -1):
            pl.semaphore_signal(barrier, inc=1, device_id=device(step, sign), device_id_type=MESH)

    loads = []

    def load(src, dst, slot):
        copy = pltpu.make_async_copy(src, dst, load_sem.at[slot])
        copy.start()
        loads.append(copy)

    load(k_hbm, kv_own.at[0], 0)
    load(v_hbm, kv_own.at[1], 1)
    for h in range(head_count):
        columns = pl.ds(h * width, width)
        load(q_hbm.at[:, columns], q_vm.at[h], 2 + 3 * h)
        load(do_hbm.at[:, columns], do_vm.at[h], 3 + 3 * h)
        load(o_hbm.at[:, columns], o_vm.at[h], 4 + 3 * h)
    for copy in loads:
        copy.wait()

    pl.semaphore_wait(barrier, 2 * len(steps))

    def kv_copy(step):
        return pltpu.make_async_remote_copy(
            src_ref=kv_own, dst_ref=kv_in.at[step - 1],
            send_sem=kv_send.at[step - 1], recv_sem=kv_recv.at[step - 1],
            device_id=device(step, 1), device_id_type=MESH)

    def g_copy(step):
        return pltpu.make_async_remote_copy(
            src_ref=g_out.at[step - 1], dst_ref=g_in.at[step - 1],
            send_sem=g_send.at[step - 1], recv_sem=g_recv.at[step - 1],
            device_id=device(step, -1), device_id_type=MESH)

    for step in STEP_ORDER:
        kv_copy(step).start()

    def spans(step):
        u, w = device(step, -1)
        block = u * outer_count + w
        return span_ref[2 * block], span_ref[2 * block + 1]

    def position(step, dim):
        first, second = spans(step)
        at = lax.broadcasted_iota(jnp.int32, (rows, rows), dim)
        return jnp.where(at < half, first * half + at, second * half + at - half)

    query_pos = position(0, 1)
    lse_row = jnp.concatenate([lse_ref[h:h + 1, :] for h in range(head_count)], axis=1)
    delta_rows = []
    for h in range(head_count):
        product = do_vm[h].astype(jnp.float32) * o_vm[h].astype(jnp.float32)
        delta_rows.append(jnp.sum(product.T, axis=0, keepdims=True))
    delta_row = jnp.concatenate(delta_rows, axis=1)
    features = head_count * rows

    def dot(x, y, dims):
        return lax.dot_general(x, y, (dims, ((), ())), preferred_element_type=jnp.float32)

    def visit(step, key_block, value_block):
        q_all = q_vm[...].reshape(features, width)
        do_all = do_vm[...].reshape(features, width)
        if step == 0:
            allowed = position(0, 0) <= query_pos
        else:
            code = code_ref[0, step - 1]
            limit = jnp.where(code == 2, jnp.int32(2 ** 31 - 1), jnp.int32(-1))
            reach = jnp.where(code == 1, query_pos, limit)
            allowed = position(step, 0) <= reach
        allowed = jnp.concatenate([allowed] * head_count, axis=1)
        scores = dot(key_block, q_all, ((1,), (1,))) * scale
        probs = jnp.where(allowed, jnp.exp(scores - lse_row), 0.0)
        dprob = dot(value_block, do_all, ((1,), (1,)))
        dscore = (probs * (dprob - delta_row) * scale).astype(jnp.bfloat16)
        value_part = dot(probs.astype(jnp.bfloat16), do_all, ((1,), (0,)))
        key_part = dot(dscore, q_all, ((1,), (0,)))
        query_part = dot(key_block.T, dscore, ((1,), (0,)))
        return query_part, key_part, value_part

    dq_acc[...], own_acc[0], own_acc[1] = visit(0, kv_own[0], kv_own[1])
    for step in STEP_ORDER:
        kv_copy(step).wait_recv()
        query_part, key_part, value_part = visit(step, kv_in[step - 1, 0], kv_in[step - 1, 1])
        g_out[step - 1, 0] = key_part.astype(jnp.bfloat16)
        g_out[step - 1, 1] = value_part.astype(jnp.bfloat16)
        g_copy(step).start()
        dq_acc[...] += query_part
    for h in range(head_count):
        columns = pl.ds(h * rows, rows)
        dq_ref[:, pl.ds(h * width, width)] = dq_acc[:, columns].T.astype(jnp.bfloat16)
    total = own_acc[...]
    for step in STEP_ORDER:
        g_copy(step).wait_recv()
        total = total + g_in[step - 1].astype(jnp.float32)
    dk_ref[...] = total[0].astype(jnp.bfloat16)
    dv_ref[...] = total[1].astype(jnp.bfloat16)
    for step in STEP_ORDER:
        kv_copy(step).wait_send()
        g_copy(step).wait_send()


def shards(queries, keys, values, out_grad, forward_out, log_sum_exp, span_table, mask_codes):
    rows, features = queries.shape
    width = keys.shape[1]
    heads = log_sum_exp.shape[0]
    remote = len(WINDOW_PATH) - 1
    hbm = pl.BlockSpec(memory_space=pl.ANY)
    vmem = pl.BlockSpec(memory_space=pltpu.VMEM)
    smem = pl.BlockSpec(memory_space=pltpu.SMEM)
    return pl.pallas_call(
        functools.partial(kernel, lax.axis_size("inner"), lax.axis_size("outer")),
        out_shape=(
            jax.ShapeDtypeStruct((rows, features), jnp.bfloat16),
            jax.ShapeDtypeStruct((rows, width), jnp.bfloat16),
            jax.ShapeDtypeStruct((rows, width), jnp.bfloat16),
        ),
        in_specs=[hbm, hbm, hbm, hbm, hbm, vmem, smem, smem],
        out_specs=(vmem, vmem, vmem),
        scratch_shapes=[
            pltpu.VMEM((heads, rows, width), jnp.bfloat16),
            pltpu.VMEM((heads, rows, width), jnp.bfloat16),
            pltpu.VMEM((heads, rows, width), jnp.bfloat16),
            pltpu.VMEM((2, rows, width), jnp.bfloat16),
            pltpu.VMEM((remote, 2, rows, width), jnp.bfloat16),
            pltpu.VMEM((remote, 2, rows, width), jnp.bfloat16),
            pltpu.VMEM((remote, 2, rows, width), jnp.bfloat16),
            pltpu.VMEM((width, heads * rows), jnp.float32),
            pltpu.VMEM((2, rows, width), jnp.float32),
            pltpu.SemaphoreType.DMA((2 + 3 * heads,)),
            pltpu.SemaphoreType.DMA((remote,)),
            pltpu.SemaphoreType.DMA((remote,)),
            pltpu.SemaphoreType.DMA((remote,)),
            pltpu.SemaphoreType.DMA((remote,)),
        ],
        compiler_params=pltpu.CompilerParams(collective_id=0, has_side_effects=True),
    )(queries, keys, values, out_grad, forward_out, log_sum_exp, span_table, mask_codes)


def solution(mesh):
    return jax.shard_map(
        shards,
        mesh=mesh,
        in_specs=(
            P(("inner", "outer"), None),
            P(("inner", "outer"), None),
            P(("inner", "outer"), None),
            P(("inner", "outer"), None),
            P(("inner", "outer"), None),
            P(None, ("inner", "outer")),
            P(),
            P(("inner", "outer"), None),
        ),
        out_specs=(
            P(("inner", "outer"), None),
            P(("inner", "outer"), None),
            P(("inner", "outer"), None),
        ),
        check_vma=False,
    )
```

```python
import functools

import jax
import jax.numpy as jnp
from jax import lax
from jax.experimental import pallas as pl
from jax.experimental.pallas import tpu as pltpu
from jax.sharding import PartitionSpec as P

WINDOW_PATH = ((0, 0), (1, 0), (2, 0), (2, 1), (3, 1), (4, 1), (4, 2))
STEP_ORDER = (1, 2, 5, 4, 3, 6)
SEND_ORDER = (3, 4, 6, 5, 2, 1)
MESH = pl.DeviceIdType.MESH


def kernel(inner_count, outer_count, q_hbm, k_hbm, v_hbm, do_hbm, o_hbm, lse_hbm, span_hbm, code_hbm,
           dq_hbm, dk_hbm, dv_hbm,
           lse_ref, span_ref, code_ref, dq_ref, sum_ref, q_vm, do_vm, o_vm, kv_own, kv_in, g_out, g_in, dq_acc, own_acc,
           load_sem, store_sem, kv_send, kv_recv, g_send, g_recv):
    inner_at = lax.axis_index("inner")
    outer_at = lax.axis_index("outer")
    head_count, rows, width = q_vm.shape
    half = rows // 2
    scale = width ** (-0.5)
    steps = range(1, len(WINDOW_PATH))

    def device(step, sign):
        a, c = WINDOW_PATH[step]
        u = lax.rem(inner_at + (sign * a) % inner_count, inner_count)
        w = lax.rem(outer_at + (sign * c) % outer_count, outer_count)
        return u, w

    barrier = pltpu.get_barrier_semaphore()
    for step in SEND_ORDER:
        pl.semaphore_signal(barrier, inc=1, device_id=device(step, -1), device_id_type=MESH)

    loads = []

    def load(src, dst, slot):
        copy = pltpu.make_async_copy(src, dst, load_sem.at[slot])
        copy.start()
        loads.append(copy)

    load(k_hbm, kv_own.at[0], 0)
    load(v_hbm, kv_own.at[1], 1)
    load(lse_hbm, lse_ref, 2 + 3 * head_count)
    load(span_hbm, span_ref, 3 + 3 * head_count)
    load(code_hbm, code_ref, 4 + 3 * head_count)
    for h in range(head_count):
        columns = pl.ds(h * width, width)
        load(q_hbm.at[:, columns], q_vm.at[h], 2 + 3 * h)
        load(do_hbm.at[:, columns], do_vm.at[h], 3 + 3 * h)
        load(o_hbm.at[:, columns], o_vm.at[h], 4 + 3 * h)
    for copy in loads[:2]:
        copy.wait()

    pl.semaphore_wait(barrier, len(steps))

    def kv_copy(step):
        return pltpu.make_async_remote_copy(
            src_ref=kv_own, dst_ref=kv_in.at[step - 1],
            send_sem=kv_send.at[step - 1], recv_sem=kv_recv.at[step - 1],
            device_id=device(step, 1), device_id_type=MESH)

    def g_copy(step):
        return pltpu.make_async_remote_copy(
            src_ref=g_out.at[step - 1], dst_ref=g_in.at[step - 1],
            send_sem=g_send.at[step - 1], recv_sem=g_recv.at[step - 1],
            device_id=device(step, -1), device_id_type=MESH)

    for step in SEND_ORDER:
        kv_copy(step).start()
    for copy in loads[2:]:
        copy.wait()

    def spans(step):
        u, w = device(step, -1)
        block = u * outer_count + w
        return span_ref[2 * block], span_ref[2 * block + 1]

    def position(step, dim):
        first, second = spans(step)
        at = lax.broadcasted_iota(jnp.int32, (rows, rows), dim)
        return jnp.where(at < half, first * half + at, second * half + at - half)

    query_pos = position(0, 1)
    lse_row = jnp.concatenate([lse_ref[h:h + 1, :] for h in range(head_count)], axis=1)
    delta_rows = []
    for h in range(head_count):
        product = do_vm[h].astype(jnp.float32) * o_vm[h].astype(jnp.float32)
        delta_rows.append(jnp.sum(product.T, axis=0, keepdims=True))
    delta_row = jnp.concatenate(delta_rows, axis=1)
    features = head_count * rows

    def dot(x, y, dims):
        return lax.dot_general(x, y, (dims, ((), ())), preferred_element_type=jnp.float32)

    def visit(step, key_block, value_block):
        q_all = q_vm[...].reshape(features, width)
        do_all = do_vm[...].reshape(features, width)
        if step == 0:
            allowed = position(0, 0) <= query_pos
        else:
            code = code_ref[0, step - 1]
            limit = jnp.where(code == 2, jnp.int32(2 ** 31 - 1), jnp.int32(-1))
            reach = jnp.where(code == 1, query_pos, limit)
            allowed = position(step, 0) <= reach
        allowed = jnp.concatenate([allowed] * head_count, axis=1)
        scores = dot(key_block, q_all, ((1,), (1,))) * scale
        probs = jnp.where(allowed, jnp.exp(scores - lse_row), 0.0)
        dprob = dot(value_block, do_all, ((1,), (1,)))
        dscore = (probs * (dprob - delta_row) * scale).astype(jnp.bfloat16)
        value_part = dot(probs.astype(jnp.bfloat16), do_all, ((1,), (0,)))
        key_part = dot(dscore, q_all, ((1,), (0,)))
        query_part = dot(key_block.T, dscore, ((1,), (0,)))
        return query_part, key_part, value_part

    dq_acc[...], own_acc[0], own_acc[1] = visit(0, kv_own[0], kv_own[1])
    for step in STEP_ORDER:
        kv_copy(step).wait_recv()
        query_part, key_part, value_part = visit(step, kv_in[step - 1, 0], kv_in[step - 1, 1])
        g_out[step - 1, 0] = key_part.astype(jnp.bfloat16)
        g_out[step - 1, 1] = value_part.astype(jnp.bfloat16)
        g_copy(step).start()
        dq_acc[...] += query_part
    for h in range(head_count):
        columns = pl.ds(h * rows, rows)
        dq_ref[:, pl.ds(h * width, width)] = dq_acc[:, columns].T.astype(jnp.bfloat16)
    dq_store = pltpu.make_async_copy(dq_ref, dq_hbm, store_sem.at[0])
    dq_store.start()
    total = own_acc[...]
    for step in STEP_ORDER:
        g_copy(step).wait_recv()
        total = total + g_in[step - 1].astype(jnp.float32)
    sum_ref[...] = total.astype(jnp.bfloat16)
    dk_store = pltpu.make_async_copy(sum_ref.at[0], dk_hbm, store_sem.at[1])
    dv_store = pltpu.make_async_copy(sum_ref.at[1], dv_hbm, store_sem.at[2])
    dk_store.start()
    dv_store.start()
    dq_store.wait()
    dk_store.wait()
    dv_store.wait()
    for step in STEP_ORDER:
        kv_copy(step).wait_send()
        g_copy(step).wait_send()


def finish(dq_in, dk_in, dv_in, dq_out, dk_out, dv_out, sem):
    moves = []
    for slot, (src, dst) in enumerate(((dq_in, dq_out), (dk_in, dk_out), (dv_in, dv_out))):
        move = pltpu.make_async_copy(src, dst, sem.at[slot])
        move.start()
        moves.append(move)
    for move in moves:
        move.wait()


def shards(queries, keys, values, out_grad, forward_out, log_sum_exp, span_table, mask_codes):
    rows, features = queries.shape
    width = keys.shape[1]
    heads = log_sum_exp.shape[0]
    remote = len(WINDOW_PATH) - 1
    hbm = pl.BlockSpec(memory_space=pl.ANY)
    vmem = pl.BlockSpec(memory_space=pltpu.VMEM)
    grads = (
        jax.ShapeDtypeStruct((rows, features), jnp.bfloat16),
        jax.ShapeDtypeStruct((rows, width), jnp.bfloat16),
        jax.ShapeDtypeStruct((rows, width), jnp.bfloat16),
    )
    parts = pl.pallas_call(
        functools.partial(kernel, lax.axis_size("inner"), lax.axis_size("outer")),
        out_shape=grads,
        in_specs=[hbm] * 8,
        out_specs=(hbm, hbm, hbm),
        scratch_shapes=[
            pltpu.VMEM((heads, rows), jnp.float32),
            pltpu.SMEM(span_table.shape, jnp.int32),
            pltpu.SMEM(mask_codes.shape, jnp.int32),
            pltpu.VMEM((rows, features), jnp.bfloat16),
            pltpu.VMEM((2, rows, width), jnp.bfloat16),
            pltpu.VMEM((heads, rows, width), jnp.bfloat16),
            pltpu.VMEM((heads, rows, width), jnp.bfloat16),
            pltpu.VMEM((heads, rows, width), jnp.bfloat16),
            pltpu.VMEM((2, rows, width), jnp.bfloat16),
            pltpu.VMEM((remote, 2, rows, width), jnp.bfloat16),
            pltpu.VMEM((remote, 2, rows, width), jnp.bfloat16),
            pltpu.VMEM((remote, 2, rows, width), jnp.bfloat16),
            pltpu.VMEM((width, heads * rows), jnp.float32),
            pltpu.VMEM((2, rows, width), jnp.float32),
            pltpu.SemaphoreType.DMA((5 + 3 * heads,)),
            pltpu.SemaphoreType.DMA((3,)),
            pltpu.SemaphoreType.DMA((remote,)),
            pltpu.SemaphoreType.DMA((remote,)),
            pltpu.SemaphoreType.DMA((remote,)),
            pltpu.SemaphoreType.DMA((remote,)),
        ],
        compiler_params=pltpu.CompilerParams(
            collective_id=0, has_side_effects=True),
    )(queries, keys, values, out_grad, forward_out, log_sum_exp, span_table, mask_codes)
    return pl.pallas_call(
        finish,
        out_shape=grads,
        in_specs=[vmem] * 3,
        out_specs=(hbm, hbm, hbm),
        scratch_shapes=[pltpu.SemaphoreType.DMA((3,))],
        compiler_params=pltpu.CompilerParams(vmem_limit_bytes=16 * 2 ** 20),
    )(*parts)


def solution(mesh):
    return jax.shard_map(
        shards,
        mesh=mesh,
        in_specs=(
            P(("inner", "outer"), None),
            P(("inner", "outer"), None),
            P(("inner", "outer"), None),
            P(("inner", "outer"), None),
            P(("inner", "outer"), None),
            P(None, ("inner", "outer")),
            P(),
            P(("inner", "outer"), None),
        ),
        out_specs=(
            P(("inner", "outer"), None),
            P(("inner", "outer"), None),
            P(("inner", "outer"), None),
        ),
        check_vma=False,
    )
```

```python
import functools

import jax
import jax.numpy as jnp
from jax import lax
from jax.experimental import pallas as pl
from jax.experimental.pallas import tpu as pltpu
from jax.sharding import PartitionSpec as P

WINDOW_PATH = ((0, 0), (1, 0), (2, 0), (2, 1), (3, 1), (4, 1), (4, 2))
STEP_ORDER = (1, 2, 5, 4, 3, 6)
DIRECT = (5, 6, 2, 1)
HUB = 5
RELAYED = (3, 4)
MESH = pl.DeviceIdType.MESH


def kernel(inner_count, outer_count, q_hbm, k_hbm, v_hbm, do_hbm, o_hbm, lse_hbm, span_hbm, code_hbm,
           dq_hbm, dk_hbm, dv_hbm,
           lse_ref, span_ref, code_ref, dq_ref, sum_ref, q_vm, do_vm, o_vm, kv_own, kv_in, g_out, g_in, dq_acc, own_acc, hub_acc,
           load_sem, store_sem, kv_send, kv_recv, g_send, g_recv):
    inner_at = lax.axis_index("inner")
    outer_at = lax.axis_index("outer")
    head_count, rows, width = q_vm.shape
    half = rows // 2
    scale = width ** (-0.5)
    steps = range(1, len(WINDOW_PATH))

    def shifted(a, c):
        u = lax.rem(inner_at + a % inner_count, inner_count)
        w = lax.rem(outer_at + c % outer_count, outer_count)
        return u, w

    def device(step, sign):
        a, c = WINDOW_PATH[step]
        return shifted(sign * a, sign * c)

    def reader(step):
        a, c = WINDOW_PATH[step]
        if step in RELAYED:
            return shifted(a - WINDOW_PATH[HUB][0], c - WINDOW_PATH[HUB][1])
        return shifted(a, c)

    def sender(step):
        a, c = WINDOW_PATH[step]
        if step in RELAYED:
            return shifted(WINDOW_PATH[HUB][0] - a, WINDOW_PATH[HUB][1] - c)
        return shifted(-a, -c)

    barrier = pltpu.get_barrier_semaphore()
    for step in DIRECT + RELAYED:
        pl.semaphore_signal(barrier, inc=1, device_id=sender(step), device_id_type=MESH)

    loads = []

    def load(src, dst, slot):
        copy = pltpu.make_async_copy(src, dst, load_sem.at[slot])
        copy.start()
        loads.append(copy)

    load(k_hbm, kv_own.at[0], 0)
    load(v_hbm, kv_own.at[1], 1)
    load(lse_hbm, lse_ref, 2 + 3 * head_count)
    load(span_hbm, span_ref, 3 + 3 * head_count)
    load(code_hbm, code_ref, 4 + 3 * head_count)
    for h in range(head_count):
        columns = pl.ds(h * width, width)
        load(q_hbm.at[:, columns], q_vm.at[h], 2 + 3 * h)
        load(do_hbm.at[:, columns], do_vm.at[h], 3 + 3 * h)
        load(o_hbm.at[:, columns], o_vm.at[h], 4 + 3 * h)
    for copy in loads[:2]:
        copy.wait()

    pl.semaphore_wait(barrier, len(steps))

    def kv_copy(step, part):
        source = kv_in.at[HUB - 1, part] if step in RELAYED else kv_own.at[part]
        return pltpu.make_async_remote_copy(
            src_ref=source, dst_ref=kv_in.at[step - 1, part],
            send_sem=kv_send.at[step - 1, part], recv_sem=kv_recv.at[step - 1, part],
            device_id=reader(step), device_id_type=MESH)

    def g_copy(step, part):
        return pltpu.make_async_remote_copy(
            src_ref=g_out.at[step - 1, part], dst_ref=g_in.at[step - 1, part],
            send_sem=g_send.at[step - 1, part], recv_sem=g_recv.at[step - 1, part],
            device_id=sender(step), device_id_type=MESH)

    for step in DIRECT:
        for part in range(2):
            kv_copy(step, part).start()
    for copy in loads[2:]:
        copy.wait()

    def spans(step):
        u, w = device(step, -1)
        block = u * outer_count + w
        return span_ref[2 * block], span_ref[2 * block + 1]

    def position(step, dim):
        first, second = spans(step)
        at = lax.broadcasted_iota(jnp.int32, (rows, rows), dim)
        return jnp.where(at < half, first * half + at, second * half + at - half)

    query_pos = position(0, 1)
    lse_row = jnp.concatenate([lse_ref[h:h + 1, :] for h in range(head_count)], axis=1)
    delta_rows = []
    for h in range(head_count):
        product = do_vm[h].astype(jnp.float32) * o_vm[h].astype(jnp.float32)
        delta_rows.append(jnp.sum(product.T, axis=0, keepdims=True))
    delta_row = jnp.concatenate(delta_rows, axis=1)
    features = head_count * rows

    def dot(x, y, dims):
        return lax.dot_general(x, y, (dims, ((), ())), preferred_element_type=jnp.float32)

    def visit(step, key_block, value_block):
        q_all = q_vm[...].reshape(features, width)
        do_all = do_vm[...].reshape(features, width)
        if step == 0:
            allowed = position(0, 0) <= query_pos
        else:
            code = code_ref[0, step - 1]
            limit = jnp.where(code == 2, jnp.int32(2 ** 31 - 1), jnp.int32(-1))
            reach = jnp.where(code == 1, query_pos, limit)
            allowed = position(step, 0) <= reach
        allowed = jnp.concatenate([allowed] * head_count, axis=1)
        scores = dot(key_block, q_all, ((1,), (1,))) * scale
        probs = jnp.where(allowed, jnp.exp(scores - lse_row), 0.0)
        dprob = dot(value_block, do_all, ((1,), (1,)))
        dscore = (probs * (dprob - delta_row) * scale).astype(jnp.bfloat16)
        value_part = dot(probs.astype(jnp.bfloat16), do_all, ((1,), (0,)))
        key_part = dot(dscore, q_all, ((1,), (0,)))
        query_part = dot(key_block.T, dscore, ((1,), (0,)))
        return query_part, key_part, value_part

    dq_acc[...], own_acc[0], own_acc[1] = visit(0, kv_own[0], kv_own[1])
    def put(step, part, value):
        g_out[step - 1, part] = value.astype(jnp.bfloat16)
        g_copy(step, part).start()

    for step in STEP_ORDER:
        for part in range(2):
            kv_copy(step, part).wait_recv()
            if step == HUB:
                for onward in RELAYED:
                    kv_copy(onward, part).start()
        query_part, key_part, value_part = visit(step, kv_in[step - 1, 0], kv_in[step - 1, 1])
        if step == HUB:
            hub_acc[0] = key_part
            hub_acc[1] = value_part
        else:
            put(step, 1, value_part)
            put(step, 0, key_part)
        dq_acc[...] += query_part
    for h in range(head_count):
        columns = pl.ds(h * rows, rows)
        dq_ref[:, pl.ds(h * width, width)] = dq_acc[:, columns].T.astype(jnp.bfloat16)
    dq_store = pltpu.make_async_copy(dq_ref, dq_hbm, store_sem.at[0])
    dq_store.start()
    for part in (1, 0):
        joined = hub_acc[part]
        for step in RELAYED:
            g_copy(step, part).wait_recv()
            joined = joined + g_in[step - 1, part].astype(jnp.float32)
        put(HUB, part, joined)
    for part in (1, 0):
        total = own_acc[part]
        for step in (1, 2, 6, HUB):
            g_copy(step, part).wait_recv()
            total = total + g_in[step - 1, part].astype(jnp.float32)
        sum_ref[part] = total.astype(jnp.bfloat16)
    dk_store = pltpu.make_async_copy(sum_ref.at[0], dk_hbm, store_sem.at[1])
    dv_store = pltpu.make_async_copy(sum_ref.at[1], dv_hbm, store_sem.at[2])
    dk_store.start()
    dv_store.start()
    dq_store.wait()
    dk_store.wait()
    dv_store.wait()
    for step in STEP_ORDER:
        for part in range(2):
            kv_copy(step, part).wait_send()
            g_copy(step, part).wait_send()


def finish(dq_in, dk_in, dv_in, dq_out, dk_out, dv_out, dq_vm, dk_vm, dv_vm, in_sem, out_sem):
    moves = []
    rows = dq_vm.shape[0]
    quarter = rows // 4
    pieces = [(dq_in, dq_vm, dq_out, pl.ds(at * quarter, quarter)) for at in range(4)]
    pieces += [(dk_in, dk_vm, dk_out, pl.ds(0, rows)), (dv_in, dv_vm, dv_out, pl.ds(0, rows))]
    for slot, (src, held, dst, part) in enumerate(pieces):
        get = pltpu.make_async_copy(src.at[part], held.at[part], in_sem.at[slot])
        get.start()
        moves.append((get, pltpu.make_async_copy(held.at[part], dst.at[part], out_sem.at[slot])))
    for get, out in moves:
        get.wait()
        out.start()
    for _, out in moves:
        out.wait()


def shards(queries, keys, values, out_grad, forward_out, log_sum_exp, span_table, mask_codes):
    rows, features = queries.shape
    width = keys.shape[1]
    heads = log_sum_exp.shape[0]
    remote = len(WINDOW_PATH) - 1
    hbm = pl.BlockSpec(memory_space=pl.ANY)
    grads = (
        jax.ShapeDtypeStruct((rows, features), jnp.bfloat16),
        jax.ShapeDtypeStruct((rows, width), jnp.bfloat16),
        jax.ShapeDtypeStruct((rows, width), jnp.bfloat16),
    )
    parts = pl.pallas_call(
        functools.partial(kernel, lax.axis_size("inner"), lax.axis_size("outer")),
        out_shape=grads,
        in_specs=[hbm] * 8,
        out_specs=(hbm, hbm, hbm),
        scratch_shapes=[
            pltpu.VMEM((heads, rows), jnp.float32),
            pltpu.SMEM(span_table.shape, jnp.int32),
            pltpu.SMEM(mask_codes.shape, jnp.int32),
            pltpu.VMEM((rows, features), jnp.bfloat16),
            pltpu.VMEM((2, rows, width), jnp.bfloat16),
            pltpu.VMEM((heads, rows, width), jnp.bfloat16),
            pltpu.VMEM((heads, rows, width), jnp.bfloat16),
            pltpu.VMEM((heads, rows, width), jnp.bfloat16),
            pltpu.VMEM((2, rows, width), jnp.bfloat16),
            pltpu.VMEM((remote, 2, rows, width), jnp.bfloat16),
            pltpu.VMEM((remote, 2, rows, width), jnp.bfloat16),
            pltpu.VMEM((remote, 2, rows, width), jnp.bfloat16),
            pltpu.VMEM((width, heads * rows), jnp.float32),
            pltpu.VMEM((2, rows, width), jnp.float32),
            pltpu.VMEM((2, rows, width), jnp.float32),
            pltpu.SemaphoreType.DMA((5 + 3 * heads,)),
            pltpu.SemaphoreType.DMA((3,)),
            pltpu.SemaphoreType.DMA((remote, 2)),
            pltpu.SemaphoreType.DMA((remote, 2)),
            pltpu.SemaphoreType.DMA((remote, 2)),
            pltpu.SemaphoreType.DMA((remote, 2)),
        ],
        compiler_params=pltpu.CompilerParams(
            collective_id=0, has_side_effects=True),
    )(queries, keys, values, out_grad, forward_out, log_sum_exp, span_table, mask_codes)
    return pl.pallas_call(
        finish,
        out_shape=grads,
        in_specs=[hbm] * 3,
        out_specs=(hbm, hbm, hbm),
        scratch_shapes=[pltpu.VMEM(grad.shape, grad.dtype) for grad in grads]
        + [pltpu.SemaphoreType.DMA((6,)), pltpu.SemaphoreType.DMA((6,))],
    )(*parts)


def solution(mesh):
    return jax.shard_map(
        shards,
        mesh=mesh,
        in_specs=(
            P(("inner", "outer"), None),
            P(("inner", "outer"), None),
            P(("inner", "outer"), None),
            P(("inner", "outer"), None),
            P(("inner", "outer"), None),
            P(None, ("inner", "outer")),
            P(),
            P(("inner", "outer"), None),
        ),
        out_specs=(
            P(("inner", "outer"), None),
            P(("inner", "outer"), None),
            P(("inner", "outer"), None),
        ),
        check_vma=False,
    )
```

```python
import functools

import jax
import jax.numpy as jnp
from jax import lax
from jax.experimental import pallas as pl
from jax.experimental.pallas import tpu as pltpu
from jax.sharding import PartitionSpec as P

WINDOW_PATH = ((0, 0), (1, 0), (2, 0), (2, 1), (3, 1), (4, 1), (4, 2))
STEP_ORDER = (1, 2, 5, 4, 3, 6)
SEND_ORDER = (3, 4, 6, 5, 2, 1)
MESH = pl.DeviceIdType.MESH


def kernel(inner_count, outer_count, q_hbm, k_hbm, v_hbm, do_hbm, o_hbm, lse_hbm, span_hbm, code_hbm,
           dq_hbm, dk_hbm, dv_hbm,
           lse_ref, span_ref, code_ref, dq_ref, sum_ref, q_vm, do_vm, o_vm, kv_own, kv_in, g_out, g_in, dq_acc, own_acc,
           load_sem, store_sem, kv_send, kv_recv, g_send, g_recv):
    inner_at = lax.axis_index("inner")
    outer_at = lax.axis_index("outer")
    head_count, rows, width = q_vm.shape
    half = rows // 2
    scale = width ** (-0.5)
    steps = range(1, len(WINDOW_PATH))

    def shifted(a, c):
        u = lax.rem(inner_at + a % inner_count, inner_count)
        w = lax.rem(outer_at + c % outer_count, outer_count)
        return u, w

    def device(step, sign):
        a, c = WINDOW_PATH[step]
        return shifted(sign * a, sign * c)

    barrier = pltpu.get_barrier_semaphore()
    for step in SEND_ORDER:
        pl.semaphore_signal(barrier, inc=1, device_id=device(step, -1), device_id_type=MESH)

    loads = []

    def load(src, dst, slot):
        copy = pltpu.make_async_copy(src, dst, load_sem.at[slot])
        copy.start()
        loads.append(copy)

    load(k_hbm, kv_own.at[0], 0)
    load(v_hbm, kv_own.at[1], 1)
    load(lse_hbm, lse_ref, 2 + 3 * head_count)
    load(span_hbm, span_ref, 3 + 3 * head_count)
    load(code_hbm, code_ref, 4 + 3 * head_count)
    for h in range(head_count):
        columns = pl.ds(h * width, width)
        load(q_hbm.at[:, columns], q_vm.at[h], 2 + 3 * h)
        load(do_hbm.at[:, columns], do_vm.at[h], 3 + 3 * h)
        load(o_hbm.at[:, columns], o_vm.at[h], 4 + 3 * h)
    for copy in loads[:2]:
        copy.wait()

    pl.semaphore_wait(barrier, len(steps))

    def kv_copy(step, part):
        return pltpu.make_async_remote_copy(
            src_ref=kv_own.at[part], dst_ref=kv_in.at[step - 1, part],
            send_sem=kv_send.at[step - 1, part], recv_sem=kv_recv.at[step - 1, part],
            device_id=device(step, 1), device_id_type=MESH)

    def g_copy(step, part):
        return pltpu.make_async_remote_copy(
            src_ref=g_out.at[step - 1, part], dst_ref=g_in.at[step - 1, part],
            send_sem=g_send.at[step - 1, part], recv_sem=g_recv.at[step - 1, part],
            device_id=device(step, -1), device_id_type=MESH)

    for step in SEND_ORDER:
        for part in range(2):
            kv_copy(step, part).start()
    for copy in loads[2:]:
        copy.wait()

    def spans(step):
        u, w = device(step, -1)
        block = u * outer_count + w
        return span_ref[2 * block], span_ref[2 * block + 1]

    def position(step, dim):
        first, second = spans(step)
        at = lax.broadcasted_iota(jnp.int32, (rows, rows), dim)
        return jnp.where(at < half, first * half + at, second * half + at - half)

    query_pos = position(0, 1)
    lse_row = jnp.concatenate([lse_ref[h:h + 1, :] for h in range(head_count)], axis=1)
    delta_rows = []
    for h in range(head_count):
        product = do_vm[h].astype(jnp.float32) * o_vm[h].astype(jnp.float32)
        delta_rows.append(jnp.sum(product.T, axis=0, keepdims=True))
    delta_row = jnp.concatenate(delta_rows, axis=1)
    features = head_count * rows

    def dot(x, y, dims):
        return lax.dot_general(x, y, (dims, ((), ())), preferred_element_type=jnp.float32)

    def visit(step, key_block, value_block):
        q_all = q_vm[...].reshape(features, width)
        do_all = do_vm[...].reshape(features, width)
        if step == 0:
            allowed = position(0, 0) <= query_pos
        else:
            code = code_ref[0, step - 1]
            limit = jnp.where(code == 2, jnp.int32(2 ** 31 - 1), jnp.int32(-1))
            reach = jnp.where(code == 1, query_pos, limit)
            allowed = position(step, 0) <= reach
        allowed = jnp.concatenate([allowed] * head_count, axis=1)
        scores = dot(key_block, q_all, ((1,), (1,))) * scale
        probs = jnp.where(allowed, jnp.exp(scores - lse_row), 0.0)
        dprob = dot(value_block, do_all, ((1,), (1,)))
        dscore = (probs * (dprob - delta_row) * scale).astype(jnp.bfloat16)
        value_part = dot(probs.astype(jnp.bfloat16), do_all, ((1,), (0,)))
        key_part = dot(dscore, q_all, ((1,), (0,)))
        query_part = dot(key_block.T, dscore, ((1,), (0,)))
        return query_part, key_part, value_part

    dq_acc[...], own_acc[0], own_acc[1] = visit(0, kv_own[0], kv_own[1])
    def put(step, part, value):
        g_out[step - 1, part] = value.astype(jnp.bfloat16)
        g_copy(step, part).start()

    for step in STEP_ORDER:
        for part in range(2):
            kv_copy(step, part).wait_recv()
        query_part, key_part, value_part = visit(step, kv_in[step - 1, 0], kv_in[step - 1, 1])
        put(step, 1, value_part)
        put(step, 0, key_part)
        dq_acc[...] += query_part
    for h in range(head_count):
        columns = pl.ds(h * rows, rows)
        dq_ref[:, pl.ds(h * width, width)] = dq_acc[:, columns].T.astype(jnp.bfloat16)
    dq_store = pltpu.make_async_copy(dq_ref, dq_hbm, store_sem.at[0])
    dq_store.start()
    for part in (1, 0):
        total = own_acc[part]
        for step in STEP_ORDER:
            g_copy(step, part).wait_recv()
            total = total + g_in[step - 1, part].astype(jnp.float32)
        sum_ref[part] = total.astype(jnp.bfloat16)
    dk_store = pltpu.make_async_copy(sum_ref.at[0], dk_hbm, store_sem.at[1])
    dv_store = pltpu.make_async_copy(sum_ref.at[1], dv_hbm, store_sem.at[2])
    dk_store.start()
    dv_store.start()
    dq_store.wait()
    dk_store.wait()
    dv_store.wait()
    for step in STEP_ORDER:
        for part in range(2):
            kv_copy(step, part).wait_send()
            g_copy(step, part).wait_send()


def finish(dq_in, dk_in, dv_in, dq_out, dk_out, dv_out, dq_vm, dk_vm, dv_vm, in_sem, out_sem):
    moves = []
    rows = dq_vm.shape[0]
    quarter = rows // 4
    pieces = [(dq_in, dq_vm, dq_out, pl.ds(at * quarter, quarter)) for at in range(4)]
    pieces += [(dk_in, dk_vm, dk_out, pl.ds(0, rows)), (dv_in, dv_vm, dv_out, pl.ds(0, rows))]
    for slot, (src, held, dst, part) in enumerate(pieces):
        get = pltpu.make_async_copy(src.at[part], held.at[part], in_sem.at[slot])
        get.start()
        moves.append((get, pltpu.make_async_copy(held.at[part], dst.at[part], out_sem.at[slot])))
    for get, out in moves:
        get.wait()
        out.start()
    for _, out in moves:
        out.wait()


def shards(queries, keys, values, out_grad, forward_out, log_sum_exp, span_table, mask_codes):
    rows, features = queries.shape
    width = keys.shape[1]
    heads = log_sum_exp.shape[0]
    remote = len(WINDOW_PATH) - 1
    hbm = pl.BlockSpec(memory_space=pl.ANY)
    grads = (
        jax.ShapeDtypeStruct((rows, features), jnp.bfloat16),
        jax.ShapeDtypeStruct((rows, width), jnp.bfloat16),
        jax.ShapeDtypeStruct((rows, width), jnp.bfloat16),
    )
    parts = pl.pallas_call(
        functools.partial(kernel, lax.axis_size("inner"), lax.axis_size("outer")),
        out_shape=grads,
        in_specs=[hbm] * 8,
        out_specs=(hbm, hbm, hbm),
        scratch_shapes=[
            pltpu.VMEM((heads, rows), jnp.float32),
            pltpu.SMEM(span_table.shape, jnp.int32),
            pltpu.SMEM(mask_codes.shape, jnp.int32),
            pltpu.VMEM((rows, features), jnp.bfloat16),
            pltpu.VMEM((2, rows, width), jnp.bfloat16),
            pltpu.VMEM((heads, rows, width), jnp.bfloat16),
            pltpu.VMEM((heads, rows, width), jnp.bfloat16),
            pltpu.VMEM((heads, rows, width), jnp.bfloat16),
            pltpu.VMEM((2, rows, width), jnp.bfloat16),
            pltpu.VMEM((remote, 2, rows, width), jnp.bfloat16),
            pltpu.VMEM((remote, 2, rows, width), jnp.bfloat16),
            pltpu.VMEM((remote, 2, rows, width), jnp.bfloat16),
            pltpu.VMEM((width, heads * rows), jnp.float32),
            pltpu.VMEM((2, rows, width), jnp.float32),
            pltpu.SemaphoreType.DMA((5 + 3 * heads,)),
            pltpu.SemaphoreType.DMA((3,)),
            pltpu.SemaphoreType.DMA((remote, 2)),
            pltpu.SemaphoreType.DMA((remote, 2)),
            pltpu.SemaphoreType.DMA((remote, 2)),
            pltpu.SemaphoreType.DMA((remote, 2)),
        ],
        compiler_params=pltpu.CompilerParams(
            collective_id=0, has_side_effects=True),
    )(queries, keys, values, out_grad, forward_out, log_sum_exp, span_table, mask_codes)
    return pl.pallas_call(
        finish,
        out_shape=grads,
        in_specs=[hbm] * 3,
        out_specs=(hbm, hbm, hbm),
        scratch_shapes=[pltpu.VMEM(grad.shape, grad.dtype) for grad in grads]
        + [pltpu.SemaphoreType.DMA((6,)), pltpu.SemaphoreType.DMA((6,))],
    )(*parts)


def solution(mesh):
    return jax.shard_map(
        shards,
        mesh=mesh,
        in_specs=(
            P(("inner", "outer"), None),
            P(("inner", "outer"), None),
            P(("inner", "outer"), None),
            P(("inner", "outer"), None),
            P(("inner", "outer"), None),
            P(None, ("inner", "outer")),
            P(),
            P(("inner", "outer"), None),
        ),
        out_specs=(
            P(("inner", "outer"), None),
            P(("inner", "outer"), None),
            P(("inner", "outer"), None),
        ),
        check_vma=False,
    )
```

```python
import functools

import jax
import jax.numpy as jnp
from jax import lax
from jax.experimental import pallas as pl
from jax.experimental.pallas import tpu as pltpu
from jax.sharding import PartitionSpec as P

WINDOW_PATH = ((0, 0), (1, 0), (2, 0), (2, 1), (3, 1), (4, 1), (4, 2))
STEP_ORDER = (1, 2, 6, 5, 4, 3)
SEND_ORDER = (3, 4, 6, 5, 2, 1)
MESH = pl.DeviceIdType.MESH


def kernel(inner_count, outer_count, q_hbm, k_hbm, v_hbm, do_hbm, o_hbm, lse_hbm, span_hbm, code_hbm,
           dq_hbm, dk_hbm, dv_hbm,
           lse_ref, span_ref, code_ref, dq_ref, sum_ref, q_vm, do_vm, o_vm, kv_own, kv_in, g_out, g_in, dq_acc, own_acc,
           load_sem, store_sem, kv_send, kv_recv, g_send, g_recv):
    inner_at = lax.axis_index("inner")
    outer_at = lax.axis_index("outer")
    head_count, rows, width = q_vm.shape
    half = rows // 2
    scale = width ** (-0.5)
    steps = range(1, len(WINDOW_PATH))

    def shifted(a, c):
        u = lax.rem(inner_at + a % inner_count, inner_count)
        w = lax.rem(outer_at + c % outer_count, outer_count)
        return u, w

    def device(step, sign):
        a, c = WINDOW_PATH[step]
        return shifted(sign * a, sign * c)

    barrier = pltpu.get_barrier_semaphore()
    for step in SEND_ORDER:
        pl.semaphore_signal(barrier, inc=1, device_id=device(step, -1), device_id_type=MESH)

    loads = []

    def load(src, dst, slot):
        copy = pltpu.make_async_copy(src, dst, load_sem.at[slot])
        copy.start()
        loads.append(copy)

    load(k_hbm, kv_own.at[0], 0)
    load(v_hbm, kv_own.at[1], 1)
    load(lse_hbm, lse_ref, 2 + 3 * head_count)
    load(span_hbm, span_ref, 3 + 3 * head_count)
    load(code_hbm, code_ref, 4 + 3 * head_count)
    for h in range(head_count):
        columns = pl.ds(h * width, width)
        load(q_hbm.at[:, columns], q_vm.at[h], 2 + 3 * h)
        load(do_hbm.at[:, columns], do_vm.at[h], 3 + 3 * h)
        load(o_hbm.at[:, columns], o_vm.at[h], 4 + 3 * h)
    for copy in loads[:2]:
        copy.wait()

    pl.semaphore_wait(barrier, len(steps))

    def kv_copy(step, part):
        return pltpu.make_async_remote_copy(
            src_ref=kv_own.at[part], dst_ref=kv_in.at[step - 1, part],
            send_sem=kv_send.at[step - 1, part], recv_sem=kv_recv.at[step - 1, part],
            device_id=device(step, 1), device_id_type=MESH)

    def g_copy(step, part):
        return pltpu.make_async_remote_copy(
            src_ref=g_out.at[step - 1, part], dst_ref=g_in.at[step - 1, part],
            send_sem=g_send.at[step - 1, part], recv_sem=g_recv.at[step - 1, part],
            device_id=device(step, -1), device_id_type=MESH)

    for step in SEND_ORDER:
        for part in range(2):
            kv_copy(step, part).start()
    for copy in loads[2:]:
        copy.wait()

    def spans(step):
        u, w = device(step, -1)
        block = u * outer_count + w
        return span_ref[2 * block], span_ref[2 * block + 1]

    def position(step, dim):
        first, second = spans(step)
        at = lax.broadcasted_iota(jnp.int32, (rows, rows), dim)
        return jnp.where(at < half, first * half + at, second * half + at - half)

    query_pos = position(0, 1)
    lse_row = jnp.concatenate([lse_ref[h:h + 1, :] for h in range(head_count)], axis=1)
    delta_rows = []
    for h in range(head_count):
        product = do_vm[h].astype(jnp.float32) * o_vm[h].astype(jnp.float32)
        delta_rows.append(jnp.sum(product.T, axis=0, keepdims=True))
    delta_row = jnp.concatenate(delta_rows, axis=1)
    features = head_count * rows

    def dot(x, y, dims):
        return lax.dot_general(x, y, (dims, ((), ())), preferred_element_type=jnp.float32)

    def visit(step, key_block, value_block):
        q_all = q_vm[...].reshape(features, width)
        do_all = do_vm[...].reshape(features, width)
        if step == 0:
            allowed = position(0, 0) <= query_pos
        else:
            code = code_ref[0, step - 1]
            limit = jnp.where(code == 2, jnp.int32(2 ** 31 - 1), jnp.int32(-1))
            reach = jnp.where(code == 1, query_pos, limit)
            allowed = position(step, 0) <= reach
        allowed = jnp.concatenate([allowed] * head_count, axis=1)
        scores = dot(key_block, q_all, ((1,), (1,))) * scale
        probs = jnp.where(allowed, jnp.exp(scores - lse_row), 0.0)
        dprob = dot(value_block, do_all, ((1,), (1,)))
        dscore = (probs * (dprob - delta_row) * scale).astype(jnp.bfloat16)
        value_part = dot(probs.astype(jnp.bfloat16), do_all, ((1,), (0,)))
        key_part = dot(dscore, q_all, ((1,), (0,)))
        query_part = dot(key_block.T, dscore, ((1,), (0,)))
        return query_part, key_part, value_part

    dq_acc[...], own_acc[0], own_acc[1] = visit(0, kv_own[0], kv_own[1])
    def put(step, part, value):
        g_out[step - 1, part] = value.astype(jnp.bfloat16)
        g_copy(step, part).start()

    for step in STEP_ORDER:
        for part in range(2):
            kv_copy(step, part).wait_recv()
        query_part, key_part, value_part = visit(step, kv_in[step - 1, 0], kv_in[step - 1, 1])
        put(step, 1, value_part)
        put(step, 0, key_part)
        dq_acc[...] += query_part
    for h in range(head_count):
        columns = pl.ds(h * rows, rows)
        dq_ref[:, pl.ds(h * width, width)] = dq_acc[:, columns].T.astype(jnp.bfloat16)
    dq_store = pltpu.make_async_copy(dq_ref, dq_hbm, store_sem.at[0])
    dq_store.start()
    dk_store = pltpu.make_async_copy(sum_ref.at[0], dk_hbm, store_sem.at[1])
    dv_store = pltpu.make_async_copy(sum_ref.at[1], dv_hbm, store_sem.at[2])
    for part, store in ((1, dv_store), (0, dk_store)):
        total = own_acc[part]
        for step in STEP_ORDER:
            g_copy(step, part).wait_recv()
            total = total + g_in[step - 1, part].astype(jnp.float32)
        sum_ref[part] = total.astype(jnp.bfloat16)
        store.start()
    dq_store.wait()
    dk_store.wait()
    dv_store.wait()
    for step in STEP_ORDER:
        for part in range(2):
            kv_copy(step, part).wait_send()
            g_copy(step, part).wait_send()


def finish(dq_in, dk_in, dv_in, dq_out, dk_out, dv_out, dq_vm, dk_vm, dv_vm, in_sem, out_sem):
    moves = []
    rows = dq_vm.shape[0]
    quarter = rows // 4
    pieces = [(dq_in, dq_vm, dq_out, pl.ds(at * quarter, quarter)) for at in range(4)]
    pieces += [(dk_in, dk_vm, dk_out, pl.ds(0, rows)), (dv_in, dv_vm, dv_out, pl.ds(0, rows))]
    for slot, (src, held, dst, part) in enumerate(pieces):
        get = pltpu.make_async_copy(src.at[part], held.at[part], in_sem.at[slot])
        get.start()
        moves.append((get, pltpu.make_async_copy(held.at[part], dst.at[part], out_sem.at[slot])))
    for get, out in moves:
        get.wait()
        out.start()
    for _, out in moves:
        out.wait()


def shards(queries, keys, values, out_grad, forward_out, log_sum_exp, span_table, mask_codes):
    rows, features = queries.shape
    width = keys.shape[1]
    heads = log_sum_exp.shape[0]
    remote = len(WINDOW_PATH) - 1
    hbm = pl.BlockSpec(memory_space=pl.ANY)
    grads = (
        jax.ShapeDtypeStruct((rows, features), jnp.bfloat16),
        jax.ShapeDtypeStruct((rows, width), jnp.bfloat16),
        jax.ShapeDtypeStruct((rows, width), jnp.bfloat16),
    )
    parts = pl.pallas_call(
        functools.partial(kernel, lax.axis_size("inner"), lax.axis_size("outer")),
        out_shape=grads,
        in_specs=[hbm] * 8,
        out_specs=(hbm, hbm, hbm),
        scratch_shapes=[
            pltpu.VMEM((heads, rows), jnp.float32),
            pltpu.SMEM(span_table.shape, jnp.int32),
            pltpu.SMEM(mask_codes.shape, jnp.int32),
            pltpu.VMEM((rows, features), jnp.bfloat16),
            pltpu.VMEM((2, rows, width), jnp.bfloat16),
            pltpu.VMEM((heads, rows, width), jnp.bfloat16),
            pltpu.VMEM((heads, rows, width), jnp.bfloat16),
            pltpu.VMEM((heads, rows, width), jnp.bfloat16),
            pltpu.VMEM((2, rows, width), jnp.bfloat16),
            pltpu.VMEM((remote, 2, rows, width), jnp.bfloat16),
            pltpu.VMEM((remote, 2, rows, width), jnp.bfloat16),
            pltpu.VMEM((remote, 2, rows, width), jnp.bfloat16),
            pltpu.VMEM((width, heads * rows), jnp.float32),
            pltpu.VMEM((2, rows, width), jnp.float32),
            pltpu.SemaphoreType.DMA((5 + 3 * heads,)),
            pltpu.SemaphoreType.DMA((3,)),
            pltpu.SemaphoreType.DMA((remote, 2)),
            pltpu.SemaphoreType.DMA((remote, 2)),
            pltpu.SemaphoreType.DMA((remote, 2)),
            pltpu.SemaphoreType.DMA((remote, 2)),
        ],
        compiler_params=pltpu.CompilerParams(
            collective_id=0, has_side_effects=True),
    )(queries, keys, values, out_grad, forward_out, log_sum_exp, span_table, mask_codes)
    return pl.pallas_call(
        finish,
        out_shape=grads,
        in_specs=[hbm] * 3,
        out_specs=(hbm, hbm, hbm),
        scratch_shapes=[pltpu.VMEM(grad.shape, grad.dtype) for grad in grads]
        + [pltpu.SemaphoreType.DMA((6,)), pltpu.SemaphoreType.DMA((6,))],
    )(*parts)


def solution(mesh):
    return jax.shard_map(
        shards,
        mesh=mesh,
        in_specs=(
            P(("inner", "outer"), None),
            P(("inner", "outer"), None),
            P(("inner", "outer"), None),
            P(("inner", "outer"), None),
            P(("inner", "outer"), None),
            P(None, ("inner", "outer")),
            P(),
            P(("inner", "outer"), None),
        ),
        out_specs=(
            P(("inner", "outer"), None),
            P(("inner", "outer"), None),
            P(("inner", "outer"), None),
        ),
        check_vma=False,
    )
```
